32 devices in a mesh: team: 2 (over core), obs: 4 (over z), grid: 4 (over y, x).
Axes of the slice: x: 2, y: 2, z: 4, core: 2. Of those that a mesh axis runs over, the one named last changes fastest.
Arguments:
- design_panel: bfloat16 [8192, 1024], P('obs', ('team', 'grid')), may hold values from -6 to 6
- design_front: bfloat16 [8192, 6144], P('obs', 'grid'), may hold values from -6 to 6
- arc_ids: int32 [8192], P('obs'), may hold values from 0 to 127
- arc_weight: float32 [128], replicated, may hold values from 0.5 to 2
- row_counts: int32 [4], P('obs'), may hold values from 128 to 2048, as said below
- panel_inverse: float32 [1024, 1024], P(('team', 'obs')), may hold values from -6.525546e-05 to 0.0020539933
- front: float32 [6144, 6144], P(('team', 'obs'), 'grid'), may hold values from -1.2 to 21.2
Outputs:
- factor_row: float32 [1024, 6144], P(('team', 'obs'), 'grid')
- front_next: float32 [6144, 6144], P(('team', 'obs'), 'grid')
The draws below stay inside these ranges and needn't reach their ends.
Inputs may be any that keep to these rules, and one draw needn't show every extreme that they name: `row_counts`: every count is a multiple of 128, and in every draw some shard's count equals 2048.
All inputs are finite; a program needn't handle non-finite values.
Results may differ from the reference program's by a relative error of at most 0.0035.
Values may be sent and summed in bfloat16 or wider, within the bound.
A program may use at most 64 MiB of HBM per device.

```python
import math
import jax
import jax.numpy as jnp
from jax import lax

B = 1024
M2 = 6144
ROW_DEV = 2048
ARCS = 128
SHARDS = 4
OBS_ROWS = 8192


def draw_row_counts(key, part):
    tiles_most = ROW_DEV // 128
    key_tiles, key_peak = jax.random.split(jax.random.fold_in(key, 11))
    picked = jax.random.randint(key_tiles, (SHARDS,), 1, tiles_most + 1)
    tile_counts = jnp.maximum(picked * picked // tiles_most, 1)
    peak_shard = jax.random.randint(key_peak, (), 0, SHARDS)
    tile_counts = jnp.where(jnp.arange(SHARDS) == peak_shard, tiles_most, tile_counts)
    return (tile_counts * 128).astype(jnp.int32)


def draw_panel_inverse(key, part):
    key_diag, key_off = jax.random.split(jax.random.fold_in(key, 23))
    overall = 0.09 / jnp.sqrt(jnp.float32(OBS_ROWS))
    diagonal = jax.random.uniform(key_diag, (B,), jnp.float32, 1.0, 2.0)
    off_diagonal = 0.7 * jnp.clip(jax.random.normal(key_off, (B, B), jnp.float32), -3.0, 3.0) / jnp.sqrt(jnp.float32(B))
    lower = jnp.tril(jnp.ones((B, B), jnp.float32), -1)
    return overall * (off_diagonal * lower + jnp.diag(diagonal))


def draw_front(key, part):
    key_sym, key_diag = jax.random.split(jax.random.fold_in(key, 37))
    noise_draw = jnp.clip(jax.random.normal(key_sym, (M2, M2), jnp.float32), -4.0, 4.0)
    symmetric = 0.15 * (noise_draw + noise_draw.T)
    diagonal = jax.random.uniform(key_diag, (M2,), jnp.float32, 12.0, 20.0)
    return symmetric + jnp.diag(diagonal)


def set_ends(values, key, least, largest):
    spot = [jax.random.randint(jax.random.fold_in(key, axis), (), 0, length) for axis, length in enumerate(values.shape)]
    main_axis = values.shape.index(max(values.shape))
    beside = spot[:main_axis] + [(spot[main_axis] + 1) % values.shape[main_axis]] + spot[main_axis + 1:]
    return values.at[tuple(spot)].set(least).at[tuple(beside)].set(largest)


def shard_levels(rng, dims, shards, low, high):
    factor_of = 1.0
    for dim, parts in shards:
        draws = jax.random.uniform(jax.random.fold_in(jax.random.fold_in(rng, 6), dim), (parts,), jnp.float32, low / len(shards), high / len(shards))
        factor_of = factor_of * jnp.repeat(jnp.exp(draws), dims[dim] // parts).reshape((-1,) + (1,) * (len(dims) - 1 - dim))
    return factor_of


def bell_draw(own_key, extent, spread, limit, cuts=(), kind=jnp.bfloat16):
    loudness = shard_levels(own_key, extent, cuts, -0.22, 0.18) if cuts else 1.0
    entries = jax.random.normal(own_key, extent, jnp.float32) * spread * loudness
    return jnp.minimum(jnp.maximum(entries, -limit), limit).astype(kind)


def setup_inputs(seed: int = 0) -> dict:
    key_list = jax.random.split(jax.random.key(seed), 8)
    return {
        "design_panel": bell_draw(key_list[0], (OBS_ROWS, B), 1.0, 6.0, ((0, 4), (1, 8))),
        "design_front": bell_draw(key_list[1], (OBS_ROWS, M2), 1.0, 6.0, ((0, 4), (1, 4))),
        "arc_ids": set_ends(jax.random.randint(key_list[2], (OBS_ROWS,), 0, ARCS), jax.random.fold_in(key_list[2], 1), 0, ARCS - 1).astype(jnp.int32),
        "arc_weight": jnp.clip(jnp.exp(jax.random.uniform(key_list[3], (ARCS,), jnp.float32, math.log(0.5), math.log(2.0))), 0.5, 2.0),
        "row_counts": draw_row_counts(jax.random.fold_in(key_list[7], 71), 0),
        "panel_inverse": draw_panel_inverse(jax.random.fold_in(key_list[7], 71), 0),
        "front": draw_front(jax.random.fold_in(key_list[7], 71), 0),
    }


def reference(design_panel, design_front, arc_ids, arc_weight, row_counts, panel_inverse, front):
    position = jnp.arange(OBS_ROWS, dtype=jnp.int32)
    shard_of = (position // ROW_DEV).astype(jnp.int32)
    within = (position % ROW_DEV).astype(jnp.int32)
    is_live = (within < row_counts[shard_of]).astype(jnp.float32)
    row_weight = arc_weight[arc_ids] * is_live
    panel_shards = design_panel.reshape(SHARDS, ROW_DEV, B)
    front_shards = design_front.reshape(SHARDS, ROW_DEV, M2)
    weight_shards = row_weight.reshape(SHARDS, ROW_DEV)

    def add_shard(running, pieces):
        panel_piece, front_piece, weight_piece = pieces
        scaled_rows = (front_piece.astype(jnp.float32) * weight_piece[:, None]).astype(jnp.bfloat16)
        return running + jnp.dot(panel_piece.T, scaled_rows, preferred_element_type=jnp.float32), None

    panel_block = lax.scan(add_shard, jnp.zeros((B, M2), jnp.float32), (panel_shards, front_shards, weight_shards))[0]
    factor_row = jnp.dot(panel_inverse, panel_block, precision=lax.Precision.HIGHEST, preferred_element_type=jnp.float32)
    update = jnp.dot(factor_row.T, factor_row, precision=lax.Precision.HIGHEST, preferred_element_type=jnp.float32)
    return factor_row, front - update
```

```python
import jax
import jax.numpy as jnp
from jax import lax
from jax.sharding import PartitionSpec as P


def live_weights(arc_ids, arc_weight, row_counts):
    row_total = arc_ids.shape[0]
    arc_total = arc_weight.shape[0]
    hit = arc_ids[:, None] == lax.broadcasted_iota(jnp.int32, (row_total, arc_total), 1)
    looked = jnp.sum(jnp.where(hit, arc_weight[None, :], 0.0), axis=1)
    is_live = lax.broadcasted_iota(jnp.int32, (row_total,), 0) < row_counts[0]
    return looked * is_live.astype(jnp.float32)


def contract_rows(left, right):
    return lax.dot_general(
        left, right, (((0,), (0,)), ((), ())), preferred_element_type=jnp.float32
    )


def local(design_panel, design_front, arc_ids, arc_weight, row_counts, panel_inverse, front):
    high = lax.reduce_precision(panel_inverse, 8, 7)
    split = jnp.concatenate([high, panel_inverse - high], axis=1).astype(jnp.bfloat16)
    inverse_whole = lax.all_gather(split, ("team", "obs"), axis=0, tiled=True)
    weights = live_weights(arc_ids, arc_weight, row_counts)
    scaled_front = (design_front.astype(jnp.float32) * weights[:, None]).astype(jnp.bfloat16)
    panel_piece = lax.all_gather(design_panel, "grid", axis=1, tiled=True)
    partial_value = contract_rows(panel_piece, scaled_front)
    slab_rows = panel_inverse.shape[0]
    place_index = lax.axis_index(("team", "obs"))
    block_part = lax.psum_scatter(partial_value, "obs", scatter_dimension=0, tiled=True)
    block_part = block_part.astype(jnp.bfloat16)
    block_whole = lax.all_gather(block_part, ("team", "obs"), axis=0, tiled=True)
    factor_cols = jnp.dot(
        inverse_whole,
        jnp.concatenate([block_whole, block_whole], axis=0),
        preferred_element_type=jnp.float32,
    )
    factor_part = lax.dynamic_slice_in_dim(factor_cols, place_index * slab_rows, slab_rows, 0)
    factor_cols = factor_cols.astype(jnp.bfloat16)
    tile_rows = front.shape[0]
    tile_ratio = factor_cols.shape[1] // tile_rows
    offset = place_index % tile_ratio * tile_rows
    own_slice = lax.dynamic_slice_in_dim(factor_cols, offset, tile_rows, 1)
    kept = jnp.where(lax.axis_index("grid") == place_index // tile_ratio, own_slice, 0)
    factor_rows = lax.psum(kept.astype(jnp.bfloat16), "grid")
    return (factor_part, front - contract_rows(factor_rows, factor_cols))


def solution(mesh):
    placed = (
        P("obs", ("team", "grid")),
        P("obs", "grid"),
        P("obs"),
        P(),
        P("obs"),
        P(("team", "obs"), None),
        P(("team", "obs"), "grid"),
    )
    return jax.shard_map(
        local,
        mesh=mesh,
        in_specs=placed,
        out_specs=(P(("team", "obs"), "grid"), P(("team", "obs"), "grid")),
        check_vma=False,
    )
```

```python
import functools

import jax
import jax.numpy as jnp
from jax import lax
from jax.experimental import pallas as pl
from jax.experimental.pallas import tpu as pltpu
from jax.sharding import PartitionSpec as P


def live_weights(arc_ids, arc_weight, row_counts):
    row_total = arc_ids.shape[0]
    arc_total = arc_weight.shape[0]
    hit = arc_ids[:, None] == lax.broadcasted_iota(jnp.int32, (row_total, arc_total), 1)
    looked = jnp.sum(jnp.where(hit, arc_weight[None, :], 0.0), axis=1)
    is_live = lax.broadcasted_iota(jnp.int32, (row_total,), 0) < row_counts[0]
    return looked * is_live.astype(jnp.float32)


def contract_rows(left, right):
    return lax.dot_general(
        left, right, (((0,), (0,)), ((), ())), preferred_element_type=jnp.float32
    )


def local(design_panel, design_front, arc_ids, arc_weight, row_counts, panel_inverse, front):
    high = lax.reduce_precision(panel_inverse, 8, 7)
    split = jnp.concatenate([high, panel_inverse - high], axis=1).astype(jnp.bfloat16)
    inverse_whole = lax.all_gather(split, ("team", "obs"), axis=0, tiled=True)
    weights = live_weights(arc_ids, arc_weight, row_counts)
    scaled_front = (design_front.astype(jnp.float32) * weights[:, None]).astype(jnp.bfloat16)
    panel_piece = lax.all_gather(design_panel, "grid", axis=1, tiled=True)
    partial_value = contract_rows(panel_piece, scaled_front)
    slab_rows = panel_inverse.shape[0]
    place_index = lax.axis_index(("team", "obs"))
    block_part = lax.psum_scatter(partial_value, "obs", scatter_dimension=0, tiled=True)
    block_part = block_part.astype(jnp.bfloat16)
    block_whole = lax.all_gather(block_part, ("team", "obs"), axis=0, tiled=True)
    factor_cols = jnp.dot(
        inverse_whole,
        jnp.concatenate([block_whole, block_whole], axis=0),
        preferred_element_type=jnp.float32,
    )
    factor_part = lax.dynamic_slice_in_dim(factor_cols, place_index * slab_rows, slab_rows, 0)
    factor_cols = factor_cols.astype(jnp.bfloat16)
    tile_rows = front.shape[0]
    tile_ratio = factor_cols.shape[1] // tile_rows
    offset = place_index % tile_ratio * tile_rows
    own_slice = lax.dynamic_slice_in_dim(factor_cols, offset, tile_rows, 1)
    kept = jnp.where(lax.axis_index("grid") == place_index // tile_ratio, own_slice, 0)
    factor_rows = lax.psum(kept.astype(jnp.bfloat16), "grid")
    return (factor_part, front - contract_rows(factor_rows, factor_cols))


MESH = pl.DeviceIdType.MESH


def exchange(
    ratio, panel, front_cols, weights, inverse_rows,
    blk, tile, inv,
    panels, scaled, outgoing, incoming, own_sum,
    local_sem, panel_send, panel_recv, sum_send, sum_recv,
    line_send, line_recv, inv_send, inv_recv,
    team_send, team_recv, team_inv_send, team_inv_recv, tile_send, tile_recv,
):
    team, z, grid = lax.axis_index("team"), lax.axis_index("obs"), lax.axis_index("grid")
    lines = blk.shape[2]
    groups = blk.shape[1]
    x, y = lax.rem(grid, 2), lax.div(grid, 2)
    beside_x = y * 2 + (1 - x)
    beside_y = (1 - y) * 2 + x
    across = (1 - y) * 2 + (1 - x)
    partner = 1 - team
    place = team * lines + z
    root, half = lax.div(place, ratio), lax.rem(place, ratio)
    per_half = lines // ratio
    root_x, root_y = lax.rem(root, 2), lax.div(root, 2)
    is_root = grid == root
    is_relay = grid == root_y * 2 + (1 - root_x)
    width = panel.shape[1]
    piece = scaled.shape[2]

    barrier = pltpu.get_barrier_semaphore()
    for peer in (beside_x, beside_y, across):
        pl.semaphore_signal(barrier, inc=1, device_id={"grid": peer}, device_id_type=MESH)
    for p in range(1, lines):
        pl.semaphore_signal(
            barrier, inc=1, device_id={"obs": lax.rem(z + p, lines)}, device_id_type=MESH
        )
    pl.semaphore_signal(barrier, inc=1, device_id={"team": partner}, device_id_type=MESH)
    pl.semaphore_wait(barrier, lines + 3)

    def remote(src, dst, send, recv, where):
        return pltpu.make_async_remote_copy(
            src_ref=src, dst_ref=dst, send_sem=send, recv_sem=recv,
            device_id=where, device_id_type=MESH,
        )

    def panel_slot(index):
        return panels.at[lax.div(index, 2), :, pl.ds(pl.multiple_of(lax.rem(index, 2) * width, width), width)]

    panel_copies = []
    for k, peer in enumerate((beside_x, beside_y, across)):
        panel_copies.append(
            remote(panel, panel_slot(grid), panel_send.at[k], panel_recv.at[k], {"grid": peer})
        )
        panel_copies[-1].start()
    own_panel = pltpu.make_async_copy(panel, panel_slot(grid), local_sem.at[0])
    own_panel.start()
    own_inv = pltpu.make_async_copy(inverse_rows, inv.at[team, z], local_sem.at[1])
    own_inv.start()

    def line_sends(ref_of, send, recv, s):
        for d, step in ((0, 1), (1, -1)):
            held = z - step * s
            ok = (held >= 0) & (held < lines) & (z + step >= 0) & (z + step < lines)
            idx = jnp.clip(held, 0, lines - 1)
            nxt = jnp.clip(z + step, 0, lines - 1)

            @pl.when(ok)
            def _():
                remote(ref_of(idx), ref_of(idx), send.at[d, s], recv.at[d, s], {"obs": nxt}).start()

    def line_waits(ref_of, send, recv, s, then):
        for d, step in ((0, 1), (1, -1)):
            came = z - step * (s + 1)

            @pl.when((came >= 0) & (came < lines))
            def _():
                idx = jnp.clip(came, 0, lines - 1)
                pltpu.make_async_copy(ref_of(idx), ref_of(idx), recv.at[d, s]).wait()
                then(idx)

    def line_drain(ref_of, send):
        for s in range(lines - 1):
            for d, step in ((0, 1), (1, -1)):
                held = z - step * s

                @pl.when((held >= 0) & (held < lines) & (z + step >= 0) & (z + step < lines))
                def _():
                    idx = jnp.clip(held, 0, lines - 1)
                    pltpu.make_async_copy(ref_of(idx), ref_of(idx), send.at[d, s]).wait()

    def inv_of(idx):
        return inv.at[team, idx]

    def inv_to_team(idx):
        remote(inv.at[team, idx], inv.at[team, idx], team_inv_send.at[idx],
               team_inv_recv.at[idx], {"team": partner}).start()

    own_inv.wait()
    line_sends(inv_of, inv_send, inv_recv, 0)
    inv_to_team(z)

    rows = panel.shape[0]
    step_rows = 256

    @pl.loop(0, rows // step_rows)
    def _(i):
        at = pl.ds(pl.multiple_of(i * step_rows, step_rows), step_rows)
        factor = weights[at, :]
        for q in range(lines):
            part = front_cols[at, q * piece:(q + 1) * piece].astype(jnp.float32)
            scaled[q, at, :] = (part * factor).astype(jnp.bfloat16)

    own_panel.wait()
    sum_copies = []
    for order in range(groups):
        g = y if order == 0 else 1 - y
        if order == 0:
            panel_copies[0].wait_recv()
        else:
            panel_copies[1].wait_recv()
            panel_copies[2].wait_recv()
            for s in range(lines - 2):
                line_waits(inv_of, inv_send, inv_recv, s, inv_to_team)
                line_sends(inv_of, inv_send, inv_recv, s + 1)
        for p in (2, 1, 3, 0):
            dest = lax.rem(z + p, lines)
            total = contract_rows(panels[g], scaled[dest])
            if p == 0:
                own_sum[order] = total
            else:
                outgoing[order, p - 1] = total.astype(jnp.bfloat16)
                copy = remote(
                    outgoing.at[order, p - 1], incoming.at[order, p - 1],
                    sum_send.at[order, p - 1], sum_recv.at[order, p - 1], {"obs": dest},
                )
                copy.start()
                sum_copies.append(copy)

    line_waits(inv_of, inv_send, inv_recv, lines - 2, inv_to_team)

    def finished(t, g, order, idx):
        @pl.when(is_root & (lax.div(idx, per_half) == half))
        def _():
            q = lax.rem(idx, per_half)
            for k, peer in ((0, beside_x), (1, beside_y)):
                remote(blk.at[t, g, idx], tile.at[t, g, q], tile_send.at[k, t, g, q],
                       tile_recv.at[t, g, q], {"grid": peer}).start()
            pltpu.make_async_copy(blk.at[t, g, idx], tile.at[t, g, q], tile_recv.at[t, g, q]).start()

    def line_done(g, order, idx):
        remote(blk.at[team, g, idx], blk.at[team, g, idx], team_send.at[g, idx],
               team_recv.at[g, idx], {"team": partner}).start()
        finished(team, g, order, idx)

    for order in range(groups):
        g = y if order == 0 else 1 - y
        total = own_sum[order]
        for p in (1, 3, 2):
            sum_copies[order * (lines - 1) + (2, 1, 3).index(p)].wait_recv()
            total = total + incoming[order, p - 1].astype(jnp.float32)
        blk[team, g, z] = total.astype(jnp.bfloat16)

        def of(idx, g=g):
            return blk.at[team, g, idx]

        line_sends(of, line_send.at[order], line_recv.at[order], 0)
        line_done(g, order, z)

    for s in range(lines - 1):
        for order in range(groups):
            g = y if order == 0 else 1 - y

            def of(idx, g=g):
                return blk.at[team, g, idx]

            line_waits(of, line_send.at[order], line_recv.at[order], s,
                       lambda idx: line_done(g, order, idx))
            if s + 1 < lines - 1:
                line_sends(of, line_send.at[order], line_recv.at[order], s + 1)

    for order in range(groups):
        g = y if order == 0 else 1 - y
        for idx in range(lines):
            pltpu.make_async_copy(
                blk.at[partner, g, idx], blk.at[partner, g, idx], team_recv.at[g, idx]
            ).wait()
            finished(partner, g, order, idx)

    for t in (team, partner):
        for order in range(groups):
            g = y if order == 0 else 1 - y
            for q in range(per_half):
                dst = tile.at[t, g, q]
                pltpu.make_async_copy(dst, dst, tile_recv.at[t, g, q]).wait()

                @pl.when(is_relay)
                def _():
                    remote(dst, dst, tile_send.at[0, t, g, q], tile_recv.at[t, g, q],
                           {"grid": beside_y}).start()

    for copy in panel_copies + sum_copies:
        copy.wait_send()
    line_drain(inv_of, inv_send)
    for order in range(groups):
        g = y if order == 0 else 1 - y
        line_drain(lambda idx: blk.at[team, g, idx], line_send.at[order])
    for idx in range(lines):
        ref = inv.at[team, idx]
        pltpu.make_async_copy(ref, ref, team_inv_send.at[idx]).wait()
        ref = inv.at[partner, idx]
        pltpu.make_async_copy(ref, ref, team_inv_recv.at[idx]).wait()
        for g in range(groups):
            ref = blk.at[team, g, idx]
            pltpu.make_async_copy(ref, ref, team_send.at[g, idx]).wait()
    for t in range(2):
        for g in range(groups):
            for q in range(per_half):
                ref = tile.at[t, g, q]

                @pl.when(is_root | is_relay)
                def _():
                    pltpu.make_async_copy(ref, ref, tile_send.at[0, t, g, q]).wait()

                @pl.when(is_root)
                def _():
                    pltpu.make_async_copy(ref, ref, tile_send.at[1, t, g, q]).wait()


def finish(spot, blk, tile, inv, front, factor_out, front_out, cols, high, low):
    pieces, blocks, size = blk.shape[1], blk.shape[0], blk.shape[2]
    piece = blk.shape[3]
    whole = blocks * size
    slab = factor_out.shape[0]

    def factor_of(source, q, r):
        total = inv[r * size:(r + 1) * size, whole:whole + 1].astype(jnp.float32)
        total = total * source[r, q].astype(jnp.float32)
        for k in range(r + 1):
            total += jnp.dot(
                inv[r * size:(r + 1) * size, k * size:(k + 1) * size], source[k, q],
                preferred_element_type=jnp.float32,
            )
        return total

    for r in range(blocks):
        for q in range(pieces):
            value = factor_of(blk, q, r)
            cols[q, r * size:(r + 1) * size, :] = value.astype(jnp.bfloat16)
            for part in range(size // slab):
                @pl.when(spot[0] == r * (size // slab) + part)
                def _():
                    factor_out[:, q * piece:(q + 1) * piece] = value[part * slab:(part + 1) * slab]
        for q in range(tile.shape[1]):
            value = factor_of(tile, q, r)
            top = value.astype(jnp.bfloat16)
            high[q, r * size:(r + 1) * size, :] = top
            low[q, r * size:(r + 1) * size, :] = (value - top.astype(jnp.float32)).astype(jnp.bfloat16)

    for h in range(tile.shape[1]):
        for q in range(pieces):
            update = contract_rows(high[h], cols[q]) + contract_rows(low[h], cols[q])
            at = (slice(h * piece, (h + 1) * piece), slice(q * piece, (q + 1) * piece))
            front_out[at] = front[at] - update


def local_kernels(lines, design_panel, design_front, arc_ids, arc_weight, row_counts, panel_inverse, front):
    bf16 = jnp.bfloat16
    weights = live_weights(arc_ids, arc_weight, row_counts)[:, None]
    slab, whole = panel_inverse.shape
    rows, width = design_panel.shape
    cols = design_front.shape[1]
    tile_rows = front.shape[0]
    ratio = cols // tile_rows
    piece = cols // lines
    groups = 2
    size = 2 * width
    place = lax.axis_index(("team", "obs"))
    top = lax.reduce_precision(panel_inverse, 8, 7)
    row_at = lax.broadcasted_iota(jnp.int32, (slab, whole), 0) + place * slab
    on_diagonal = lax.broadcasted_iota(jnp.int32, (slab, whole), 1) == row_at
    rest = jnp.sum(jnp.where(on_diagonal, panel_inverse - top, 0.0), axis=1, keepdims=True)
    inverse_rows = jnp.concatenate(
        [top, jnp.broadcast_to(rest, (slab, 128))], axis=1
    ).astype(bf16)
    vmem = pl.BlockSpec(memory_space=pltpu.VMEM)
    dma = pltpu.SemaphoreType.DMA
    hops = lines - 1
    halves = lines // ratio
    blk, tile, inv = pl.pallas_call(
        functools.partial(exchange, ratio),
        out_shape=(
            jax.ShapeDtypeStruct((2, groups, lines, size, piece), bf16),
            jax.ShapeDtypeStruct((2, groups, halves, size, piece), bf16),
            jax.ShapeDtypeStruct((2, lines) + inverse_rows.shape, bf16),
        ),
        in_specs=[vmem] * 4,
        out_specs=(vmem,) * 3,
        scratch_shapes=[
            pltpu.VMEM((groups, rows, size), bf16),
            pltpu.VMEM((lines, rows, piece), bf16),
            pltpu.VMEM((groups, hops, size, piece), bf16),
            pltpu.VMEM((groups, hops, size, piece), bf16),
            pltpu.VMEM((groups, size, piece), jnp.float32),
            dma((2,)), dma((3,)), dma((3,)),
            dma((groups, hops)), dma((groups, hops)),
            dma((groups, 2, hops)), dma((groups, 2, hops)),
            dma((2, hops)), dma((2, hops)),
            dma((groups, lines)), dma((groups, lines)),
            dma((lines,)), dma((lines,)),
            dma((2, 2, groups, halves)), dma((2, groups, halves)),
        ],
        compiler_params=pltpu.CompilerParams(
            collective_id=0, has_side_effects=True, vmem_limit_bytes=48 * 2**20
        ),
        name="exchange",
    )(design_panel, design_front, weights, inverse_rows)
    blk = blk.reshape((2 * groups, lines, size, piece))
    tile = tile.reshape((2 * groups, halves, size, piece))
    inv = inv.reshape((whole, inverse_rows.shape[1]))
    return pl.pallas_call(
        finish,
        out_shape=(
            jax.ShapeDtypeStruct((slab, cols), jnp.float32),
            jax.ShapeDtypeStruct(front.shape, jnp.float32),
        ),
        in_specs=[pl.BlockSpec(memory_space=pltpu.SMEM)] + [vmem] * 4,
        out_specs=(vmem, vmem),
        scratch_shapes=[
            pltpu.VMEM((lines, whole, piece), bf16),
            pltpu.VMEM((halves, whole, piece), bf16),
            pltpu.VMEM((halves, whole, piece), bf16),
        ],
        compiler_params=pltpu.CompilerParams(vmem_limit_bytes=48 * 2**20),
        name="finish",
    )(place.astype(jnp.int32)[None], blk, tile, inv, front)


def solution(mesh):
    placed = (
        P("obs", ("team", "grid")),
        P("obs", "grid"),
        P("obs"),
        P(),
        P("obs"),
        P(("team", "obs"), None),
        P(("team", "obs"), "grid"),
    )
    sizes = mesh.shape
    fits = sizes["team"] == 2 and sizes["obs"] == 4 and sizes["grid"] == 4
    return jax.shard_map(
        functools.partial(local_kernels, sizes["obs"]) if fits else local,
        mesh=mesh,
        in_specs=placed,
        out_specs=(P(("team", "obs"), "grid"), P(("team", "obs"), "grid")),
        check_vma=False,
    )
```

```python
import functools

import jax
import jax.numpy as jnp
from jax import lax
from jax.experimental import pallas as pl
from jax.experimental.pallas import tpu as pltpu
from jax.sharding import PartitionSpec as P


def live_weights(arc_ids, arc_weight, row_counts):
    row_total = arc_ids.shape[0]
    arc_total = arc_weight.shape[0]
    hit = arc_ids[:, None] == lax.broadcasted_iota(jnp.int32, (row_total, arc_total), 1)
    looked = jnp.sum(jnp.where(hit, arc_weight[None, :], 0.0), axis=1)
    is_live = lax.broadcasted_iota(jnp.int32, (row_total,), 0) < row_counts[0]
    return looked * is_live.astype(jnp.float32)


def contract_rows(left, right):
    return lax.dot_general(
        left, right, (((0,), (0,)), ((), ())), preferred_element_type=jnp.float32
    )


def local(design_panel, design_front, arc_ids, arc_weight, row_counts, panel_inverse, front):
    high = lax.reduce_precision(panel_inverse, 8, 7)
    split = jnp.concatenate([high, panel_inverse - high], axis=1).astype(jnp.bfloat16)
    inverse_whole = lax.all_gather(split, ("team", "obs"), axis=0, tiled=True)
    weights = live_weights(arc_ids, arc_weight, row_counts)
    scaled_front = (design_front.astype(jnp.float32) * weights[:, None]).astype(jnp.bfloat16)
    panel_piece = lax.all_gather(design_panel, "grid", axis=1, tiled=True)
    partial_value = contract_rows(panel_piece, scaled_front)
    slab_rows = panel_inverse.shape[0]
    place_index = lax.axis_index(("team", "obs"))
    block_part = lax.psum_scatter(partial_value, "obs", scatter_dimension=0, tiled=True)
    block_part = block_part.astype(jnp.bfloat16)
    block_whole = lax.all_gather(block_part, ("team", "obs"), axis=0, tiled=True)
    factor_cols = jnp.dot(
        inverse_whole,
        jnp.concatenate([block_whole, block_whole], axis=0),
        preferred_element_type=jnp.float32,
    )
    factor_part = lax.dynamic_slice_in_dim(factor_cols, place_index * slab_rows, slab_rows, 0)
    factor_cols = factor_cols.astype(jnp.bfloat16)
    tile_rows = front.shape[0]
    tile_ratio = factor_cols.shape[1] // tile_rows
    offset = place_index % tile_ratio * tile_rows
    own_slice = lax.dynamic_slice_in_dim(factor_cols, offset, tile_rows, 1)
    kept = jnp.where(lax.axis_index("grid") == place_index // tile_ratio, own_slice, 0)
    factor_rows = lax.psum(kept.astype(jnp.bfloat16), "grid")
    return (factor_part, front - contract_rows(factor_rows, factor_cols))


MESH = pl.DeviceIdType.MESH


def exchange(
    ratio, panel, front_cols, weights, inverse_rows,
    blk, tile, inv,
    panels, scaled, outgoing, incoming, own_sum,
    local_sem, panel_send, panel_recv, sum_send, sum_recv,
    line_send, line_recv, inv_send, inv_recv,
    team_send, team_recv, inv_team_send, inv_team_recv, inv_grid_send, inv_grid_recv, tile_send, tile_recv,
):
    team, z, grid = lax.axis_index("team"), lax.axis_index("obs"), lax.axis_index("grid")
    lines = blk.shape[2]
    groups = blk.shape[1]
    x, y = lax.rem(grid, 2), lax.div(grid, 2)
    beside_x = y * 2 + (1 - x)
    beside_y = (1 - y) * 2 + x
    across = (1 - y) * 2 + (1 - x)
    partner = 1 - team
    place = team * lines + z
    root, half = lax.div(place, ratio), lax.rem(place, ratio)
    per_half = lines // ratio
    root_x, root_y = lax.rem(root, 2), lax.div(root, 2)
    is_root = grid == root
    is_relay = grid == root_y * 2 + (1 - root_x)
    width = panel.shape[1]
    piece = scaled.shape[2]

    barrier = pltpu.get_barrier_semaphore()
    for peer in (beside_x, beside_y, across):
        pl.semaphore_signal(barrier, inc=1, device_id={"grid": peer}, device_id_type=MESH)
    for p in range(1, lines):
        pl.semaphore_signal(
            barrier, inc=1, device_id={"obs": lax.rem(z + p, lines)}, device_id_type=MESH
        )
    pl.semaphore_signal(barrier, inc=1, device_id={"team": partner}, device_id_type=MESH)
    pl.semaphore_wait(barrier, lines + 3)

    def remote(src, dst, send, recv, where):
        return pltpu.make_async_remote_copy(
            src_ref=src, dst_ref=dst, send_sem=send, recv_sem=recv,
            device_id=where, device_id_type=MESH,
        )

    def panel_slot(index):
        return panels.at[lax.div(index, 2), :, pl.ds(pl.multiple_of(lax.rem(index, 2) * width, width), width)]

    panel_copies = []
    for k, peer in enumerate((beside_x, beside_y)):
        panel_copies.append(
            remote(panel, panel_slot(grid), panel_send.at[k], panel_recv.at[k], {"grid": peer})
        )
        panel_copies[-1].start()
    rows = panel.shape[0]
    middle = rows // 2
    for k, (source, peer) in enumerate(((beside_x, beside_y), (beside_y, beside_x))):
        cut = panel_slot(source).at[pl.ds(k * middle, middle)]
        panel_copies.append(
            remote(cut, cut, panel_send.at[2 + k], panel_recv.at[2 + k], {"grid": peer})
        )
    own_panel = pltpu.make_async_copy(panel, panel_slot(grid), local_sem.at[0])
    own_panel.start()
    share = inv.shape[3]
    own_rows = inverse_rows.at[pl.ds(pl.multiple_of(grid * share, share), share)]
    own_inv = pltpu.make_async_copy(own_rows, inv.at[team, z, grid], local_sem.at[1])
    own_inv.start()

    def line_sends(ref_of, send, recv, s):
        for d, step in ((0, 1), (1, -1)):
            held = z - step * s
            ok = (held >= 0) & (held < lines) & (z + step >= 0) & (z + step < lines)
            idx = jnp.clip(held, 0, lines - 1)
            nxt = jnp.clip(z + step, 0, lines - 1)

            @pl.when(ok)
            def _():
                remote(ref_of(idx), ref_of(idx), send.at[d, s], recv.at[d, s], {"obs": nxt}).start()

    def line_waits(ref_of, send, recv, s, then):
        for d, step in ((0, 1), (1, -1)):
            came = z - step * (s + 1)

            @pl.when((came >= 0) & (came < lines))
            def _():
                idx = jnp.clip(came, 0, lines - 1)
                pltpu.make_async_copy(ref_of(idx), ref_of(idx), recv.at[d, s]).wait()
                then(idx)

    def line_drain(ref_of, send):
        for s in range(lines - 1):
            for d, step in ((0, 1), (1, -1)):
                held = z - step * s

                @pl.when((held >= 0) & (held < lines) & (z + step >= 0) & (z + step < lines))
                def _():
                    idx = jnp.clip(held, 0, lines - 1)
                    pltpu.make_async_copy(ref_of(idx), ref_of(idx), send.at[d, s]).wait()

    def inv_of(idx):
        return inv.at[team, idx, grid]

    def nothing(idx):
        pass

    own_inv.wait()
    line_sends(inv_of, inv_send, inv_recv, 0)

    step_rows = 256

    @pl.loop(0, rows // step_rows)
    def _(i):
        at = pl.ds(pl.multiple_of(i * step_rows, step_rows), step_rows)
        factor = weights[at, :]
        for q in range(lines):
            part = front_cols[at, q * piece:(q + 1) * piece].astype(jnp.float32)
            scaled[q, at, :] = (part * factor).astype(jnp.bfloat16)

    own_panel.wait()
    sum_copies = []
    for order in range(groups):
        g = y if order == 0 else 1 - y
        if order == 0:
            for s in range(lines - 2):
                line_waits(inv_of, inv_send, inv_recv, s, nothing)
                line_sends(inv_of, inv_send, inv_recv, s + 1)
            panel_copies[0].wait_recv()
            panel_copies[2].start()
            panel_copies[1].wait_recv()
            panel_copies[3].start()
        else:
            panel_copies[2].wait_recv()
            panel_copies[3].wait_recv()
        for p in (2, 1, 3, 0):
            dest = lax.rem(z + p, lines)
            total = contract_rows(panels[g], scaled[dest])
            if p == 0:
                own_sum[order] = total
            else:
                outgoing[order, p - 1] = total.astype(jnp.bfloat16)
                copy = remote(
                    outgoing.at[order, p - 1], incoming.at[order, p - 1],
                    sum_send.at[order, p - 1], sum_recv.at[order, p - 1], {"obs": dest},
                )
                copy.start()
                sum_copies.append(copy)

    line_waits(inv_of, inv_send, inv_recv, lines - 2, nothing)
    inv_copies = []
    for k, peer in enumerate((beside_x, beside_y, across)):
        own = inv.at[team, :, grid]
        inv_copies.append(remote(own, own, inv_grid_send.at[k], inv_grid_recv.at[k], {"grid": peer}))
        inv_copies[-1].start()

    def finished(t, g, order, idx):
        @pl.when(is_root & (lax.div(idx, per_half) == half))
        def _():
            q = lax.rem(idx, per_half)
            for k, peer in ((0, beside_x), (1, beside_y)):
                remote(blk.at[t, g, idx], tile.at[t, g, q], tile_send.at[k, t, g, q],
                       tile_recv.at[t, g, q], {"grid": peer}).start()
            pltpu.make_async_copy(blk.at[t, g, idx], tile.at[t, g, q], tile_recv.at[t, g, q]).start()

    def line_done(g, order, idx):
        remote(blk.at[team, g, idx], blk.at[team, g, idx], team_send.at[g, idx],
               team_recv.at[g, idx], {"team": partner}).start()
        finished(team, g, order, idx)

    for order in range(groups):
        g = y if order == 0 else 1 - y
        total = own_sum[order]
        for p in (1, 3, 2):
            sum_copies[order * (lines - 1) + (2, 1, 3).index(p)].wait_recv()
            total = total + incoming[order, p - 1].astype(jnp.float32)
        blk[team, g, z] = total.astype(jnp.bfloat16)

        def of(idx, g=g):
            return blk.at[team, g, idx]

        line_sends(of, line_send.at[order], line_recv.at[order], 0)
        line_done(g, order, z)

    def settle(idx):
        for order in range(groups):
            g = y if order == 0 else 1 - y
            pltpu.make_async_copy(
                blk.at[partner, g, idx], blk.at[partner, g, idx], team_recv.at[g, idx]
            ).wait()
            finished(partner, g, order, idx)

    def relay(idx):
        for t in (team, partner):
            for order in range(groups):
                g = y if order == 0 else 1 - y

                @pl.when(is_relay & (lax.div(idx, per_half) == half))
                def _():
                    q = lax.rem(idx, per_half)
                    dst = tile.at[t, g, q]
                    pltpu.make_async_copy(dst, dst, tile_recv.at[t, g, q]).wait()
                    remote(dst, dst, tile_send.at[0, t, g, q], tile_recv.at[t, g, q],
                           {"grid": beside_y}).start()

    def each_at(s, then):
        if s < 0:
            then(z)
            return
        for step in (1, -1):
            came = z - step * (s + 1)

            @pl.when((came >= 0) & (came < lines))
            def _():
                then(jnp.clip(came, 0, lines - 1))

    for s in range(lines - 1):
        for order in range(groups):
            g = y if order == 0 else 1 - y

            def of(idx, g=g):
                return blk.at[team, g, idx]

            line_waits(of, line_send.at[order], line_recv.at[order], s,
                       lambda idx: line_done(g, order, idx))
            if s + 1 < lines - 1:
                line_sends(of, line_send.at[order], line_recv.at[order], s + 1)
        if s == 0:
            for copy in inv_copies:
                copy.wait_recv()
            inv_team = remote(inv.at[team], inv.at[team], inv_team_send, inv_team_recv, {"team": partner})
            inv_team.start()
        each_at(s - 1, settle)
        if s > 0:
            each_at(s - 2, relay)
    each_at(lines - 2, settle)
    each_at(lines - 3, relay)
    each_at(lines - 2, relay)

    for t in (team, partner):
        for order in range(groups):
            g = y if order == 0 else 1 - y
            for q in range(per_half):
                dst = tile.at[t, g, q]

                @pl.when(jnp.logical_not(is_relay))
                def _():
                    pltpu.make_async_copy(dst, dst, tile_recv.at[t, g, q]).wait()

    inv_team.wait()
    for copy in panel_copies + sum_copies + inv_copies:
        copy.wait_send()
    line_drain(inv_of, inv_send)
    for order in range(groups):
        g = y if order == 0 else 1 - y
        line_drain(lambda idx: blk.at[team, g, idx], line_send.at[order])
    for idx in range(lines):
        for g in range(groups):
            ref = blk.at[team, g, idx]
            pltpu.make_async_copy(ref, ref, team_send.at[g, idx]).wait()
    for t in range(2):
        for g in range(groups):
            for q in range(per_half):
                ref = tile.at[t, g, q]

                @pl.when(is_root | is_relay)
                def _():
                    pltpu.make_async_copy(ref, ref, tile_send.at[0, t, g, q]).wait()

                @pl.when(is_root)
                def _():
                    pltpu.make_async_copy(ref, ref, tile_send.at[1, t, g, q]).wait()


def finish(spot, blk, tile, inv, front, factor_out, front_out, cols, high, low):
    pieces, blocks, size = blk.shape[1], blk.shape[0], blk.shape[2]
    piece = blk.shape[3]
    whole = blocks * size
    slab = factor_out.shape[0]

    def factor_of(source, q, r):
        total = inv[r * size:(r + 1) * size, whole:whole + 1].astype(jnp.float32)
        total = total * source[r, q].astype(jnp.float32)
        for k in range(r + 1):
            total += jnp.dot(
                inv[r * size:(r + 1) * size, k * size:(k + 1) * size], source[k, q],
                preferred_element_type=jnp.float32,
            )
        return total

    for r in range(blocks):
        for q in range(pieces):
            value = factor_of(blk, q, r)
            cols[q, r * size:(r + 1) * size, :] = value.astype(jnp.bfloat16)
            for part in range(size // slab):
                @pl.when(spot[0] == r * (size // slab) + part)
                def _():
                    factor_out[:, q * piece:(q + 1) * piece] = value[part * slab:(part + 1) * slab]
        for q in range(tile.shape[1]):
            value = factor_of(tile, q, r)
            top = value.astype(jnp.bfloat16)
            high[q, r * size:(r + 1) * size, :] = top
            low[q, r * size:(r + 1) * size, :] = (value - top.astype(jnp.float32)).astype(jnp.bfloat16)

    for h in range(tile.shape[1]):
        for q in range(pieces):
            update = contract_rows(high[h], cols[q]) + contract_rows(low[h], cols[q])
            at = (slice(h * piece, (h + 1) * piece), slice(q * piece, (q + 1) * piece))
            front_out[at] = front[at] - update


def local_kernels(lines, grids, design_panel, design_front, arc_ids, arc_weight, row_counts, panel_inverse, front):
    bf16 = jnp.bfloat16
    weights = live_weights(arc_ids, arc_weight, row_counts)[:, None]
    slab, whole = panel_inverse.shape
    rows, width = design_panel.shape
    cols = design_front.shape[1]
    tile_rows = front.shape[0]
    ratio = cols // tile_rows
    piece = cols // lines
    groups = 2
    size = 2 * width
    place = lax.axis_index(("team", "obs"))
    top = lax.reduce_precision(panel_inverse, 8, 7)
    row_at = lax.broadcasted_iota(jnp.int32, (slab, whole), 0) + place * slab
    on_diagonal = lax.broadcasted_iota(jnp.int32, (slab, whole), 1) == row_at
    rest = jnp.sum(jnp.where(on_diagonal, panel_inverse - top, 0.0), axis=1, keepdims=True)
    inverse_rows = jnp.concatenate(
        [top, jnp.broadcast_to(rest, (slab, 128))], axis=1
    ).astype(bf16)
    vmem = pl.BlockSpec(memory_space=pltpu.VMEM)
    dma = pltpu.SemaphoreType.DMA
    hops = lines - 1
    halves = lines // ratio
    blk, tile, inv = pl.pallas_call(
        functools.partial(exchange, ratio),
        out_shape=(
            jax.ShapeDtypeStruct((2, groups, lines, size, piece), bf16),
            jax.ShapeDtypeStruct((2, groups, halves, size, piece), bf16),
            jax.ShapeDtypeStruct((2, lines, grids, slab // grids, inverse_rows.shape[1]), bf16),
        ),
        in_specs=[vmem] * 4,
        out_specs=(vmem,) * 3,
        scratch_shapes=[
            pltpu.VMEM((groups, rows, size), bf16),
            pltpu.VMEM((lines, rows, piece), bf16),
            pltpu.VMEM((groups, hops, size, piece), bf16),
            pltpu.VMEM((groups, hops, size, piece), bf16),
            pltpu.VMEM((groups, size, piece), jnp.float32),
            dma((2,)), dma((4,)), dma((4,)),
            dma((groups, hops)), dma((groups, hops)),
            dma((groups, 2, hops)), dma((groups, 2, hops)),
            dma((2, hops)), dma((2, hops)),
            dma((groups, lines)), dma((groups, lines)),
            dma, dma, dma((3,)), dma((3,)),
            dma((2, 2, groups, halves)), dma((2, groups, halves)),
        ],
        compiler_params=pltpu.CompilerParams(
            collective_id=0, has_side_effects=True, vmem_limit_bytes=48 * 2**20
        ),
        name="exchange",
    )(design_panel, design_front, weights, inverse_rows)
    blk = blk.reshape((2 * groups, lines, size, piece))
    tile = tile.reshape((2 * groups, halves, size, piece))
    inv = inv.reshape((whole, inverse_rows.shape[1]))
    return pl.pallas_call(
        finish,
        out_shape=(
            jax.ShapeDtypeStruct((slab, cols), jnp.float32),
            jax.ShapeDtypeStruct(front.shape, jnp.float32),
        ),
        in_specs=[pl.BlockSpec(memory_space=pltpu.SMEM)] + [vmem] * 4,
        out_specs=(vmem, vmem),
        scratch_shapes=[
            pltpu.VMEM((lines, whole, piece), bf16),
            pltpu.VMEM((halves, whole, piece), bf16),
            pltpu.VMEM((halves, whole, piece), bf16),
        ],
        compiler_params=pltpu.CompilerParams(vmem_limit_bytes=48 * 2**20),
        name="finish",
    )(place.astype(jnp.int32)[None], blk, tile, inv, front)


def solution(mesh):
    placed = (
        P("obs", ("team", "grid")),
        P("obs", "grid"),
        P("obs"),
        P(),
        P("obs"),
        P(("team", "obs"), None),
        P(("team", "obs"), "grid"),
    )
    sizes = mesh.shape
    fits = sizes["team"] == 2 and sizes["obs"] == 4 and sizes["grid"] == 4
    return jax.shard_map(
        functools.partial(local_kernels, sizes["obs"], sizes["grid"]) if fits else local,
        mesh=mesh,
        in_specs=placed,
        out_specs=(P(("team", "obs"), "grid"), P(("team", "obs"), "grid")),
        check_vma=False,
    )
```

```python
import functools

import jax
import jax.numpy as jnp
from jax import lax
from jax.experimental import pallas as pl
from jax.experimental.pallas import tpu as pltpu
from jax.sharding import PartitionSpec as P


def live_weights(arc_ids, arc_weight, row_counts):
    row_total = arc_ids.shape[0]
    arc_total = arc_weight.shape[0]
    hit = arc_ids[:, None] == lax.broadcasted_iota(jnp.int32, (row_total, arc_total), 1)
    looked = jnp.sum(jnp.where(hit, arc_weight[None, :], 0.0), axis=1)
    is_live = lax.broadcasted_iota(jnp.int32, (row_total,), 0) < row_counts[0]
    return looked * is_live.astype(jnp.float32)


def contract_rows(left, right):
    return lax.dot_general(
        left, right, (((0,), (0,)), ((), ())), preferred_element_type=jnp.float32
    )


def local(design_panel, design_front, arc_ids, arc_weight, row_counts, panel_inverse, front):
    high = lax.reduce_precision(panel_inverse, 8, 7)
    split = jnp.concatenate([high, panel_inverse - high], axis=1).astype(jnp.bfloat16)
    inverse_whole = lax.all_gather(split, ("team", "obs"), axis=0, tiled=True)
    weights = live_weights(arc_ids, arc_weight, row_counts)
    scaled_front = (design_front.astype(jnp.float32) * weights[:, None]).astype(jnp.bfloat16)
    panel_piece = lax.all_gather(design_panel, "grid", axis=1, tiled=True)
    partial_value = contract_rows(panel_piece, scaled_front)
    slab_rows = panel_inverse.shape[0]
    place_index = lax.axis_index(("team", "obs"))
    block_part = lax.psum_scatter(partial_value, "obs", scatter_dimension=0, tiled=True)
    block_part = block_part.astype(jnp.bfloat16)
    block_whole = lax.all_gather(block_part, ("team", "obs"), axis=0, tiled=True)
    factor_cols = jnp.dot(
        inverse_whole,
        jnp.concatenate([block_whole, block_whole], axis=0),
        preferred_element_type=jnp.float32,
    )
    factor_part = lax.dynamic_slice_in_dim(factor_cols, place_index * slab_rows, slab_rows, 0)
    factor_cols = factor_cols.astype(jnp.bfloat16)
    tile_rows = front.shape[0]
    tile_ratio = factor_cols.shape[1] // tile_rows
    offset = place_index % tile_ratio * tile_rows
    own_slice = lax.dynamic_slice_in_dim(factor_cols, offset, tile_rows, 1)
    kept = jnp.where(lax.axis_index("grid") == place_index // tile_ratio, own_slice, 0)
    factor_rows = lax.psum(kept.astype(jnp.bfloat16), "grid")
    return (factor_part, front - contract_rows(factor_rows, factor_cols))


MESH = pl.DeviceIdType.MESH


def exchange(
    ratio, panel, front_cols, weights, inverse_rows,
    blk, tile, inv,
    panels, scaled, outgoing, incoming, own_sum,
    local_sem, panel_send, panel_recv, sum_send, sum_recv,
    line_send, line_recv, inv_send, inv_recv,
    team_send, team_recv, inv_team_send, inv_team_recv, inv_grid_send, inv_grid_recv, tile_send, tile_recv,
):
    team, z, grid = lax.axis_index("team"), lax.axis_index("obs"), lax.axis_index("grid")
    lines = blk.shape[2]
    groups = blk.shape[1]
    x, y = lax.rem(grid, 2), lax.div(grid, 2)
    beside_x = y * 2 + (1 - x)
    beside_y = (1 - y) * 2 + x
    across = (1 - y) * 2 + (1 - x)
    partner = 1 - team
    place = team * lines + z
    root, half = lax.div(place, ratio), lax.rem(place, ratio)
    per_half = lines // ratio
    root_x, root_y = lax.rem(root, 2), lax.div(root, 2)
    is_root = grid == root
    is_relay = grid == root_y * 2 + (1 - root_x)
    width = panel.shape[1]
    piece = scaled.shape[2]

    barrier = pltpu.get_barrier_semaphore()
    for peer in (beside_x, beside_y, across):
        pl.semaphore_signal(barrier, inc=1, device_id={"grid": peer}, device_id_type=MESH)
    for p in range(1, lines):
        pl.semaphore_signal(
            barrier, inc=1, device_id={"obs": lax.rem(z + p, lines)}, device_id_type=MESH
        )
    pl.semaphore_signal(barrier, inc=1, device_id={"team": partner}, device_id_type=MESH)
    pl.semaphore_wait(barrier, lines + 3)

    def remote(src, dst, send, recv, where):
        return pltpu.make_async_remote_copy(
            src_ref=src, dst_ref=dst, send_sem=send, recv_sem=recv,
            device_id=where, device_id_type=MESH,
        )

    def panel_slot(index):
        return panels.at[lax.div(index, 2), :, pl.ds(pl.multiple_of(lax.rem(index, 2) * width, width), width)]

    panel_copies = []
    for k, peer in enumerate((beside_x, beside_y)):
        panel_copies.append(
            remote(panel, panel_slot(grid), panel_send.at[k], panel_recv.at[k], {"grid": peer})
        )
        panel_copies[-1].start()
    rows = panel.shape[0]
    middle = rows // 2
    for k, (source, peer) in enumerate(((beside_x, beside_y), (beside_y, beside_x))):
        cut = panel_slot(source).at[pl.ds(k * middle, middle)]
        panel_copies.append(
            remote(cut, cut, panel_send.at[2 + k], panel_recv.at[2 + k], {"grid": peer})
        )
    own_panel = pltpu.make_async_copy(panel, panel_slot(grid), local_sem.at[0])
    own_panel.start()
    share = inv.shape[3]
    own_rows = inverse_rows.at[pl.ds(pl.multiple_of(grid * share, share), share)]
    own_inv = pltpu.make_async_copy(own_rows, inv.at[team, z, grid], local_sem.at[1])
    own_inv.start()

    def line_sends(ref_of, send, recv, s):
        for d, step in ((0, 1), (1, -1)):
            held = z - step * s
            ok = (held >= 0) & (held < lines) & (z + step >= 0) & (z + step < lines)
            idx = jnp.clip(held, 0, lines - 1)
            nxt = jnp.clip(z + step, 0, lines - 1)

            @pl.when(ok)
            def _():
                remote(ref_of(idx), ref_of(idx), send.at[d, s], recv.at[d, s], {"obs": nxt}).start()

    def line_waits(ref_of, send, recv, s, then):
        for d, step in ((0, 1), (1, -1)):
            came = z - step * (s + 1)

            @pl.when((came >= 0) & (came < lines))
            def _():
                idx = jnp.clip(came, 0, lines - 1)
                pltpu.make_async_copy(ref_of(idx), ref_of(idx), recv.at[d, s]).wait()
                then(idx)

    def line_drain(ref_of, send):
        for s in range(lines - 1):
            for d, step in ((0, 1), (1, -1)):
                held = z - step * s

                @pl.when((held >= 0) & (held < lines) & (z + step >= 0) & (z + step < lines))
                def _():
                    idx = jnp.clip(held, 0, lines - 1)
                    pltpu.make_async_copy(ref_of(idx), ref_of(idx), send.at[d, s]).wait()

    def inv_of(idx):
        return inv.at[team, idx, grid]

    def nothing(idx):
        pass

    own_inv.wait()
    line_sends(inv_of, inv_send, inv_recv, 0)

    step_rows = 256

    @pl.loop(0, rows // step_rows)
    def _(i):
        at = pl.ds(pl.multiple_of(i * step_rows, step_rows), step_rows)
        factor = weights[at, :]
        for q in range(lines):
            part = front_cols[at, q * piece:(q + 1) * piece].astype(jnp.float32)
            scaled[q, at, :] = (part * factor).astype(jnp.bfloat16)

    own_panel.wait()
    sum_copies = []
    for order in range(groups):
        g = y if order == 0 else 1 - y
        if order == 0:
            for s in range(lines - 2):
                line_waits(inv_of, inv_send, inv_recv, s, nothing)
                line_sends(inv_of, inv_send, inv_recv, s + 1)
            panel_copies[0].wait_recv()
            panel_copies[2].start()
            panel_copies[1].wait_recv()
            panel_copies[3].start()
        else:
            panel_copies[2].wait_recv()
            panel_copies[3].wait_recv()
        for p in (2, 1, 3, 0):
            dest = lax.rem(z + p, lines)
            total = contract_rows(panels[g], scaled[dest])
            if p == 0:
                own_sum[order] = total
            else:
                outgoing[order, p - 1] = total.astype(jnp.bfloat16)
                copy = remote(
                    outgoing.at[order, p - 1], incoming.at[order, p - 1],
                    sum_send.at[order, p - 1], sum_recv.at[order, p - 1], {"obs": dest},
                )
                copy.start()
                sum_copies.append(copy)

    line_waits(inv_of, inv_send, inv_recv, lines - 2, nothing)
    inv_copies = []
    for k, peer in enumerate((beside_x, beside_y, across)):
        own = inv.at[team, :, grid]
        inv_copies.append(remote(own, own, inv_grid_send.at[k], inv_grid_recv.at[k], {"grid": peer}))
        inv_copies[-1].start()

    def finished(t, g, order, idx):
        @pl.when(is_root & (lax.div(idx, per_half) == half))
        def _():
            q = lax.rem(idx, per_half)
            for k, peer in ((0, beside_x), (1, beside_y)):
                remote(blk.at[t, g, idx], tile.at[t, g, q], tile_send.at[k, t, g, q],
                       tile_recv.at[t, g, q], {"grid": peer}).start()
            pltpu.make_async_copy(blk.at[t, g, idx], tile.at[t, g, q], tile_recv.at[t, g, q]).start()

    def line_done(g, order, idx):
        remote(blk.at[team, g, idx], blk.at[team, g, idx], team_send.at[g, idx],
               team_recv.at[g, idx], {"team": partner}).start()
        finished(team, g, order, idx)

    for order in range(groups):
        g = y if order == 0 else 1 - y
        total = own_sum[order]
        for p in (1, 3, 2):
            sum_copies[order * (lines - 1) + (2, 1, 3).index(p)].wait_recv()
            total = total + incoming[order, p - 1].astype(jnp.float32)
        blk[team, g, z] = total.astype(jnp.bfloat16)

        def of(idx, g=g):
            return blk.at[team, g, idx]

        line_sends(of, line_send.at[order], line_recv.at[order], 0)
        line_done(g, order, z)

    def settle(idx):
        for order in range(groups):
            g = y if order == 0 else 1 - y
            pltpu.make_async_copy(
                blk.at[partner, g, idx], blk.at[partner, g, idx], team_recv.at[g, idx]
            ).wait()
            finished(partner, g, order, idx)

    def relay(idx):
        for t in (team, partner):
            for order in range(groups):
                g = y if order == 0 else 1 - y

                @pl.when(is_relay & (lax.div(idx, per_half) == half))
                def _():
                    q = lax.rem(idx, per_half)
                    dst = tile.at[t, g, q]
                    pltpu.make_async_copy(dst, dst, tile_recv.at[t, g, q]).wait()
                    remote(dst, dst, tile_send.at[0, t, g, q], tile_recv.at[t, g, q],
                           {"grid": beside_y}).start()

    def each_at(s, then):
        if s < 0:
            then(z)
            return
        for step in (1, -1):
            came = z - step * (s + 1)

            @pl.when((came >= 0) & (came < lines))
            def _():
                then(jnp.clip(came, 0, lines - 1))

    for s in range(lines - 1):
        for order in range(groups):
            g = y if order == 0 else 1 - y

            def of(idx, g=g):
                return blk.at[team, g, idx]

            line_waits(of, line_send.at[order], line_recv.at[order], s,
                       lambda idx: line_done(g, order, idx))
            if s + 1 < lines - 1:
                line_sends(of, line_send.at[order], line_recv.at[order], s + 1)
        if s == 0:
            for copy in inv_copies:
                copy.wait_recv()
            inv_team = remote(inv.at[team], inv.at[team], inv_team_send, inv_team_recv, {"team": partner})
            inv_team.start()
        each_at(s - 1, settle)
        if s > 0:
            each_at(s - 2, relay)
    each_at(lines - 2, settle)
    each_at(lines - 3, relay)
    each_at(lines - 2, relay)

    for t in (team, partner):
        for order in range(groups):
            g = y if order == 0 else 1 - y
            for q in range(per_half):
                dst = tile.at[t, g, q]

                @pl.when(jnp.logical_not(is_relay))
                def _():
                    pltpu.make_async_copy(dst, dst, tile_recv.at[t, g, q]).wait()

    inv_team.wait()
    for copy in panel_copies + sum_copies + inv_copies:
        copy.wait_send()
    line_drain(inv_of, inv_send)
    for order in range(groups):
        g = y if order == 0 else 1 - y
        line_drain(lambda idx: blk.at[team, g, idx], line_send.at[order])
    for idx in range(lines):
        for g in range(groups):
            ref = blk.at[team, g, idx]
            pltpu.make_async_copy(ref, ref, team_send.at[g, idx]).wait()
    for t in range(2):
        for g in range(groups):
            for q in range(per_half):
                ref = tile.at[t, g, q]

                @pl.when(is_root | is_relay)
                def _():
                    pltpu.make_async_copy(ref, ref, tile_send.at[0, t, g, q]).wait()

                @pl.when(is_root)
                def _():
                    pltpu.make_async_copy(ref, ref, tile_send.at[1, t, g, q]).wait()


def finish(spot, blk, tile, inv, front, factor_out, front_out, cols, high, low, held, sems):
    pieces, blocks, size = blk.shape[1], blk.shape[0], blk.shape[2]
    piece = blk.shape[3]
    whole = blocks * size
    slab = factor_out.shape[0]

    load = pltpu.make_async_copy(front, held, sems.at[0])
    load.start()

    def factor_of(source, q, r):
        total = inv[r * size:(r + 1) * size, whole:whole + 1].astype(jnp.float32)
        total = total * source[r, q].astype(jnp.float32)
        for k in range(r + 1):
            total += jnp.dot(
                inv[r * size:(r + 1) * size, k * size:(k + 1) * size], source[k, q],
                preferred_element_type=jnp.float32,
            )
        return total

    for r in range(blocks):
        for q in range(pieces):
            value = factor_of(blk, q, r)
            cols[q, r * size:(r + 1) * size, :] = value.astype(jnp.bfloat16)
            for part in range(size // slab):
                @pl.when(spot[0] == r * (size // slab) + part)
                def _():
                    factor_out[:, q * piece:(q + 1) * piece] = value[part * slab:(part + 1) * slab]
        for q in range(tile.shape[1]):
            value = factor_of(tile, q, r)
            value = value.T
            top = value.astype(jnp.bfloat16)
            high[q, :, r * size:(r + 1) * size] = top
            low[q, :, r * size:(r + 1) * size] = (value - top.astype(jnp.float32)).astype(jnp.bfloat16)

    load.wait()
    stores = []
    for h in range(tile.shape[1]):
        for q in range(pieces):
            update = jnp.dot(high[h], cols[q], preferred_element_type=jnp.float32)
            update += jnp.dot(low[h], cols[q], preferred_element_type=jnp.float32)
            at = (pl.ds(h * piece, piece), pl.ds(q * piece, piece))
            held[at] = held[at] - update
            stores.append(
                pltpu.make_async_copy(held.at[at], front_out.at[at], sems.at[1 + h * pieces + q])
            )
            stores[-1].start()
    for store in stores:
        store.wait()


def local_kernels(lines, grids, design_panel, design_front, arc_ids, arc_weight, row_counts, panel_inverse, front):
    bf16 = jnp.bfloat16
    weights = live_weights(arc_ids, arc_weight, row_counts)[:, None]
    slab, whole = panel_inverse.shape
    rows, width = design_panel.shape
    cols = design_front.shape[1]
    tile_rows = front.shape[0]
    ratio = cols // tile_rows
    piece = cols // lines
    groups = 2
    size = 2 * width
    place = lax.axis_index(("team", "obs"))
    top = lax.reduce_precision(panel_inverse, 8, 7)
    row_at = lax.broadcasted_iota(jnp.int32, (slab, whole), 0) + place * slab
    on_diagonal = lax.broadcasted_iota(jnp.int32, (slab, whole), 1) == row_at
    rest = jnp.sum(jnp.where(on_diagonal, panel_inverse - top, 0.0), axis=1, keepdims=True)
    inverse_rows = jnp.concatenate(
        [top, jnp.broadcast_to(rest, (slab, 128))], axis=1
    ).astype(bf16)
    vmem = pl.BlockSpec(memory_space=pltpu.VMEM)
    dma = pltpu.SemaphoreType.DMA
    hops = lines - 1
    halves = lines // ratio
    blk, tile, inv = pl.pallas_call(
        functools.partial(exchange, ratio),
        out_shape=(
            jax.ShapeDtypeStruct((2, groups, lines, size, piece), bf16),
            jax.ShapeDtypeStruct((2, groups, halves, size, piece), bf16),
            jax.ShapeDtypeStruct((2, lines, grids, slab // grids, inverse_rows.shape[1]), bf16),
        ),
        in_specs=[vmem] * 4,
        out_specs=(vmem,) * 3,
        scratch_shapes=[
            pltpu.VMEM((groups, rows, size), bf16),
            pltpu.VMEM((lines, rows, piece), bf16),
            pltpu.VMEM((groups, hops, size, piece), bf16),
            pltpu.VMEM((groups, hops, size, piece), bf16),
            pltpu.VMEM((groups, size, piece), jnp.float32),
            dma((2,)), dma((4,)), dma((4,)),
            dma((groups, hops)), dma((groups, hops)),
            dma((groups, 2, hops)), dma((groups, 2, hops)),
            dma((2, hops)), dma((2, hops)),
            dma((groups, lines)), dma((groups, lines)),
            dma, dma, dma((3,)), dma((3,)),
            dma((2, 2, groups, halves)), dma((2, groups, halves)),
        ],
        compiler_params=pltpu.CompilerParams(
            collective_id=0, has_side_effects=True, vmem_limit_bytes=48 * 2**20
        ),
        name="exchange",
    )(design_panel, design_front, weights, inverse_rows)
    blk = blk.reshape((2 * groups, lines, size, piece))
    tile = tile.reshape((2 * groups, halves, size, piece))
    inv = inv.reshape((whole, inverse_rows.shape[1]))
    return pl.pallas_call(
        finish,
        out_shape=(
            jax.ShapeDtypeStruct((slab, cols), jnp.float32),
            jax.ShapeDtypeStruct(front.shape, jnp.float32),
        ),
        in_specs=[pl.BlockSpec(memory_space=pltpu.SMEM)] + [vmem] * 3 + [pl.BlockSpec(memory_space=pl.ANY)],
        out_specs=(vmem, pl.BlockSpec(memory_space=pl.ANY)),
        scratch_shapes=[
            pltpu.VMEM((lines, whole, piece), bf16),
            pltpu.VMEM((halves, piece, whole), bf16),
            pltpu.VMEM((halves, piece, whole), bf16),
            pltpu.VMEM(front.shape, jnp.float32),
            dma((1 + halves * lines,)),
        ],
        compiler_params=pltpu.CompilerParams(vmem_limit_bytes=48 * 2**20),
        name="finish",
    )(place.astype(jnp.int32)[None], blk, tile, inv, front)


def solution(mesh):
    placed = (
        P("obs", ("team", "grid")),
        P("obs", "grid"),
        P("obs"),
        P(),
        P("obs"),
        P(("team", "obs"), None),
        P(("team", "obs"), "grid"),
    )
    sizes = mesh.shape
    fits = sizes["team"] == 2 and sizes["obs"] == 4 and sizes["grid"] == 4
    return jax.shard_map(
        functools.partial(local_kernels, sizes["obs"], sizes["grid"]) if fits else local,
        mesh=mesh,
        in_specs=placed,
        out_specs=(P(("team", "obs"), "grid"), P(("team", "obs"), "grid")),
        check_vma=False,
    )
```
